32 devices in a mesh: seq: 8 (over y, x, core), fsdp: 4 (over z).
Axes of the slice: x: 2, y: 2, z: 4, core: 2. Of those that a mesh axis runs over, the one named last changes fastest.
Arguments:
- hidden: bfloat16 [8192, 3584], P(('seq', 'fsdp')), may hold values from -6 to 6
- queries: bfloat16 [8192, 2048], P(('seq', 'fsdp')), may hold values from -360 to 360
- kv_weights: bfloat16 [2, 3584, 1024], P(None, 'fsdp'), may hold values from -0.09375 to 0.09375
- image_groups: int32 [8], P('seq'), may hold values 0 or 1
- doc_ids: int32 [8192], replicated, may hold values from 0 to 7, never falling along the last dimension, each value on 1 to 3072 neighbouring positions
Outputs:
- attended: bfloat16 [8192, 2048], P(('seq', 'fsdp'))
The draws below stay inside these ranges and needn't reach their ends.
Inputs may be any that keep to these rules, and one draw needn't show every extreme that they name: `image_groups`: 1 marks a group of image tokens. `doc_ids`: never falling along the tokens; every document has 1 to 3072 tokens and one has exactly that many.
All inputs are finite; a program needn't handle non-finite values.
Results may differ from the reference program's by a relative error of at most 0.0055.
The reference program's roundings to bfloat16 on the way (of `keys_values` and `weights`) count: a program that leaves them out, or rounds other values in their place, can miss the bound.
Values may be sent and summed in bfloat16 or wider, within the bound.
A program may use at most 128 MiB of HBM per device.

```python
import math
import jax
import jax.numpy as jnp
import numpy as np
from jax import lax

D = 3584
KVH = 4
HD = 128
QH = 16
ROWS = 256
SPAN = 3
TOKENS = 8192
DOCS = 8
N_SEQ = 8
N_FSDP = 4


def draw_queries(key, part):
    base = jnp.clip(jax.random.normal(key, (TOKENS, QH * HD), jnp.float32), -6.0, 6.0)
    return base.astype(jnp.bfloat16)


def set_ends(array, own_key, smallest, high):
    index_at = [jax.random.randint(jax.random.fold_in(own_key, axis), (), 0, length) for axis, length in enumerate(array.shape)]
    longest = array.shape.index(max(array.shape))
    neighbour = index_at[:longest] + [(index_at[longest] + 1) % array.shape[longest]] + index_at[longest + 1:]
    return array.at[tuple(index_at)].set(smallest).at[tuple(neighbour)].set(high)


def levels(key, extent, cuts, smallest, top_value):
    loudness, own = 1.0, jax.random.fold_in(key, 6)
    for axis_at, shards_of in cuts:
        heights = jnp.exp(jax.random.uniform(jax.random.fold_in(own, axis_at), (shards_of,), jnp.float32, smallest / len(cuts), top_value / len(cuts)))
        loudness = loudness * jnp.repeat(heights, extent[axis_at] // shards_of).reshape([-1 if axis == axis_at else 1 for axis in range(len(extent))])
    return loudness


def profile(count, total, most, slope):
    loads = [(1 << 20) // math.isqrt(rank ** slope) + 1 for rank in range(2, count + 1)]
    surplus, given = total - most - (count - 1), [1] * (count - 1)
    while surplus > 0:
        movable = [i for i in range(count - 1) if given[i] < most]
        pool, budget = sum([loads[i] for i in movable]), surplus
        for i in movable:
            more = min(most - given[i], max(1, budget * loads[i] // pool), surplus)
            given[i] = given[i] + more
            surplus = surplus - more
    return np.array([most] + given)


def uneven_parts(rng, number_of, total, bound, skew):
    if number_of == 2:
        one = jax.random.randint(rng, (), max(1, total - bound), min(bound, total - 1) + 1)
        return jnp.stack([one, total - one])
    tallies = jnp.asarray(profile(number_of, total, bound, skew), jnp.int32)
    couples = (number_of - 1) // 2
    donor, sink = tallies[1:1 + 2 * couples:2], tallies[2:2 + 2 * couples:2]
    margin = jnp.minimum(donor - 1, bound - sink)
    passed = jax.random.randint(jax.random.fold_in(rng, 1), (couples,), 0, 1 << 20) % (margin + 1)
    tallies = tallies.at[1:1 + 2 * couples:2].set(donor - passed).at[2:2 + 2 * couples:2].set(sink + passed)
    return tallies[jax.random.permutation(jax.random.fold_in(rng, 2), number_of)]


def centred(rng, extent, deviation, most, pieces=(), kind=jnp.bfloat16):
    drawn = deviation * jax.random.normal(rng, extent, jnp.float32)
    if pieces:
        drawn = drawn * levels(rng, extent, pieces, -0.22, 0.18)
    return jnp.clip(drawn, -most, most).astype(kind)


def setup_inputs(seed: int = 0) -> dict:
    keys = jax.random.split(jax.random.key(seed), 6)
    hidden = centred(keys[0], (TOKENS, D), 1.0, 6.0, ((0, 32),))
    queries = draw_queries(jax.random.fold_in(keys[5], 71), 0)
    kv_weights = centred(keys[2], (2, D, 2 * KVH * HD), D ** -0.5, 0.09375, ((1, 4),))
    image_groups = set_ends((jax.random.randint(keys[3], (N_SEQ,), 0, 3) < 1).astype(jnp.int32), jax.random.fold_in(keys[3], 1), 0, 1)
    doc_ids = jnp.searchsorted(jnp.cumsum(uneven_parts(keys[4], DOCS, TOKENS, SPAN * ROWS * N_FSDP, 2)), jnp.arange(TOKENS), side="right").astype(jnp.int32)
    return {"hidden": hidden, "queries": queries, "kv_weights": kv_weights, "image_groups": image_groups, "doc_ids": doc_ids}


def build_mask(query_pos, key_pos, doc_ids, is_image, own_start):
    key_doc = jnp.where(key_pos >= 0, doc_ids[jnp.maximum(key_pos, 0)], -1)
    query_doc = doc_ids[query_pos]
    same_doc = query_doc[:, None] == key_doc[None, :]
    earlier = key_pos[None, :] <= query_pos[:, None]
    own_image = jnp.logical_and(is_image, key_pos[None, :] >= own_start)
    return jnp.logical_and(same_doc, jnp.logical_or(earlier, own_image))

def attend(query_rows, keys_values, allowed):
    n_query = query_rows.shape[0]
    n_keys = keys_values.shape[0]
    per_group = QH // KVH
    score_scale = 1.0 / math.sqrt(HD)
    query_heads = query_rows.reshape(n_query, KVH, per_group, HD).transpose(1, 0, 2, 3)
    key_heads = keys_values[:, :KVH * HD].reshape(n_keys, KVH, HD).transpose(1, 0, 2)
    value_heads = keys_values[:, KVH * HD:].reshape(n_keys, KVH, HD).transpose(1, 0, 2)

    def one_head(operands):
        head_q, head_k, head_v = operands
        scores = jnp.einsum('rgd,kd->grk', head_q.astype(jnp.float32), head_k.astype(jnp.float32)) * score_scale
        scores = jnp.where(allowed[None], scores, -1e+30)
        highest = lax.optimization_barrier(jnp.max(scores, axis=-1, keepdims=True))
        weights = jnp.where(allowed[None], jnp.exp(scores - highest), 0.0)
        totals = lax.optimization_barrier(jnp.sum(weights, axis=-1))
        rounded = lax.optimization_barrier(weights.astype(jnp.bfloat16))
        summed = jnp.einsum('grk,kd->rgd', rounded.astype(jnp.float32), head_v.astype(jnp.float32))
        return (summed / jnp.transpose(totals)[:, :, None]).astype(jnp.bfloat16)
    mixed = lax.map(one_head, (query_heads, key_heads, value_heads))
    return mixed.transpose(1, 0, 2, 3).reshape(n_query, QH * HD)

def reference(hidden, queries, kv_weights, image_groups, doc_ids):
    block_len = TOKENS // N_SEQ
    kv_width = 2 * KVH * HD

    def project(group):
        block_hidden = lax.dynamic_slice_in_dim(hidden, group * block_len, block_len, 0)
        weight = lax.dynamic_index_in_dim(kv_weights, image_groups[group], 0, keepdims=False)
        return jnp.dot(block_hidden, weight, preferred_element_type=jnp.float32).astype(jnp.bfloat16)
    kv_blocks = lax.map(project, jnp.arange(N_SEQ, dtype=jnp.int32))
    padded = jnp.concatenate([jnp.zeros((SPAN, block_len, kv_width), kv_blocks.dtype), kv_blocks], 0)

    def one_block(group):
        query_rows = lax.dynamic_slice_in_dim(queries, group * block_len, block_len, 0)
        window = lax.dynamic_slice_in_dim(padded, group, SPAN + 1, 0).reshape((SPAN + 1) * block_len, kv_width)
        offsets = group - SPAN + jnp.arange(SPAN + 1, dtype=jnp.int32)
        key_pos = (offsets[:, None] * block_len + jnp.arange(block_len, dtype=jnp.int32)[None, :]).reshape(-1)
        query_pos = group * block_len + jnp.arange(block_len, dtype=jnp.int32)
        allowed = build_mask(query_pos, key_pos, doc_ids, image_groups[group] == 1, group * block_len)
        return attend(query_rows, window, allowed)
    attended = lax.map(one_block, jnp.arange(N_SEQ, dtype=jnp.int32))
    return attended.reshape(TOKENS, QH * HD)
```

```python
import functools
import math

import jax
import jax.numpy as jnp
from jax import lax
from jax.experimental import pallas as pl
from jax.experimental.pallas import tpu as pltpu
from jax.sharding import PartitionSpec as P

KVH = 4
HD = 128
QH = 16
SPAN = 3
NEG = -1e30


def from_behind(block, axis, distance):
    devices = range(lax.axis_size(axis))
    route = [(i - distance, i) for i in devices if i - distance in devices]
    return lax.ppermute(block, axis, route)


def attend_kernel(key_block, marks, lo_ref, hi_ref, q_ref, k_ref, v_ref, out_ref, qt, top, total, acc):
    rows = q_ref.shape[0]
    per_group = QH // KVH
    factor = math.log2(math.e) / math.sqrt(HD)
    for g in range(per_group):
        qt[:, g * rows : (g + 1) * rows] = q_ref[:, g * HD : (g + 1) * HD].T
    top[...] = jnp.full_like(top, NEG)
    total[...] = jnp.zeros_like(total)
    acc[...] = jnp.zeros_like(acc)

    def step(masked, b, _):
        at = pl.multiple_of(b * key_block, key_block)
        keys = k_ref[pl.ds(at, key_block), :]
        values = v_ref[pl.ds(at, key_block), :]
        if masked:
            place = at + lax.broadcasted_iota(jnp.int32, (key_block, rows), 0)
            allowed = jnp.logical_and(place >= lo_ref[...], place <= hi_ref[...])
        for g in range(per_group):
            lanes = slice(g * rows, (g + 1) * rows)
            scores = jnp.dot(keys, qt[:, lanes], preferred_element_type=jnp.float32)
            if masked:
                scores = jnp.where(allowed, scores, NEG)
            before = top[:, lanes]
            peak = jnp.maximum(before, jnp.max(scores, axis=0, keepdims=True))
            weights = jnp.exp2((scores - peak) * factor)
            shrink = jnp.exp2((before - peak) * factor)
            top[:, lanes] = peak
            total[:, lanes] = total[:, lanes] * shrink + jnp.sum(weights, axis=0, keepdims=True)
            acc[:, lanes] = acc[:, lanes] * shrink + lax.dot_general(
                values,
                weights.astype(jnp.bfloat16),
                (((0,), (0,)), ((), ())),
                preferred_element_type=jnp.float32,
            )
        return 0

    first, full_first, full_end, end = marks[0], marks[1], marks[2], marks[3]
    lax.fori_loop(first, full_first, functools.partial(step, True), 0)
    lax.fori_loop(full_first, full_end, functools.partial(step, False), 0)
    lax.fori_loop(full_end, end, functools.partial(step, True), 0)
    for g in range(per_group):
        lanes = slice(g * rows, (g + 1) * rows)
        mixed = (acc[:, lanes] / total[:, lanes]).T
        out_ref[:, g * HD : (g + 1) * HD] = mixed.astype(out_ref.dtype)


def attend(queries, window, lo, hi):
    rows = queries.shape[0]
    n_keys = window.shape[0]
    key_block = math.gcd(n_keys, 512)
    per_group = QH // KVH
    lo_min, lo_max, hi_min, hi_max = jnp.min(lo), jnp.max(lo), jnp.min(hi), jnp.max(hi)
    first = lo_min // key_block
    end = hi_max // key_block + 1
    full_first = jnp.minimum((lo_max + key_block - 1) // key_block, end)
    full_end = jnp.maximum((hi_min + 1) // key_block, full_first)
    marks = jnp.stack([first, full_first, full_end, end]).astype(jnp.int32)
    wide = per_group * HD
    return pl.pallas_call(
        functools.partial(attend_kernel, key_block),
        grid=(KVH,),
        in_specs=[
            pl.BlockSpec(memory_space=pltpu.SMEM),
            pl.BlockSpec((1, rows), lambda h: (0, 0)),
            pl.BlockSpec((1, rows), lambda h: (0, 0)),
            pl.BlockSpec((rows, wide), lambda h: (0, h)),
            pl.BlockSpec((n_keys, HD), lambda h: (0, h)),
            pl.BlockSpec((n_keys, HD), lambda h: (0, KVH + h)),
        ],
        out_specs=pl.BlockSpec((rows, wide), lambda h: (0, h)),
        out_shape=jax.ShapeDtypeStruct(queries.shape, queries.dtype),
        scratch_shapes=[
            pltpu.VMEM((HD, per_group * rows), jnp.bfloat16),
            pltpu.VMEM((1, per_group * rows), jnp.float32),
            pltpu.VMEM((1, per_group * rows), jnp.float32),
            pltpu.VMEM((HD, per_group * rows), jnp.float32),
        ],
        name="attend",
    )(marks, lo[None, :], hi[None, :], queries, window, window)


def key_range(doc_ids, rows, block_rows, seq_place, fsdp_place, modality):
    start = seq_place * block_rows + fsdp_place * rows
    here = lax.dynamic_slice_in_dim(doc_ids, start, rows, 0)
    query_pos = start + jnp.arange(rows, dtype=jnp.int32)
    below = jnp.sum((doc_ids[None, :] < here[:, None]).astype(jnp.int32), axis=1)
    upto = jnp.sum((doc_ids[None, :] <= here[:, None]).astype(jnp.int32), axis=1)
    last = jnp.minimum(upto - 1, (seq_place + 1) * block_rows - 1)
    base = (seq_place - SPAN) * block_rows
    lo = below - base
    hi = jnp.where(modality == 1, last, query_pos) - base
    return lo, hi


def local(hidden, queries, kv_weights, image_groups, doc_ids):
    rows = hidden.shape[0]
    block_rows = rows * lax.axis_size("fsdp")
    seq_place = lax.axis_index("seq")
    fsdp_place = lax.axis_index("fsdp")
    modality = image_groups[0]
    lo, hi = key_range(doc_ids, rows, block_rows, seq_place, fsdp_place, modality)
    own_weight = lax.dynamic_index_in_dim(kv_weights, modality, 0, keepdims=False)
    own_kv = jnp.dot(
        hidden,
        lax.all_gather(own_weight, "fsdp", axis=0, tiled=True),
        preferred_element_type=jnp.float32,
    ).astype(jnp.bfloat16)
    block_kv = lax.all_gather(own_kv, "fsdp", axis=0, tiled=True)
    pieces = [from_behind(block_kv, "seq", offset) for offset in range(SPAN, 0, -1)]
    window = jnp.concatenate(pieces + [block_kv], 0)
    return attend(queries, window, lo, hi)


def solution(mesh):
    in_specs = (
        P(("seq", "fsdp"), None),
        P(("seq", "fsdp"), None),
        P(None, "fsdp", None),
        P("seq"),
        P(),
    )
    out_specs = P(("seq", "fsdp"), None)
    return jax.shard_map(local, mesh=mesh, in_specs=in_specs, out_specs=out_specs, check_vma=False)
```

```python
import functools
import math

import jax
import jax.numpy as jnp
from jax import lax
from jax.experimental import pallas as pl
from jax.experimental.pallas import tpu as pltpu
from jax.sharding import PartitionSpec as P

KVH = 4
HD = 128
QH = 16
SPAN = 3
NEG = -1e30


def from_behind(block, axis, distance):
    devices = range(lax.axis_size(axis))
    route = [(i - distance, i) for i in devices if i - distance in devices]
    return lax.ppermute(block, axis, route)


def attend_kernel(key_block, marks, lo_ref, hi_ref, q_ref, k_ref, v_ref, out_ref, qt, top, total, acc):
    rows = q_ref.shape[0]
    per_group = QH // KVH
    factor = math.log2(math.e) / math.sqrt(HD)
    for g in range(per_group):
        qt[:, g * rows : (g + 1) * rows] = q_ref[:, g * HD : (g + 1) * HD].T
    top[...] = jnp.full_like(top, NEG)
    total[...] = jnp.zeros_like(total)
    acc[...] = jnp.zeros_like(acc)

    def step(masked, b, _):
        at = pl.multiple_of(b * key_block, key_block)
        keys = k_ref[pl.ds(at, key_block), :]
        values = v_ref[pl.ds(at, key_block), :]
        if masked:
            place = at + lax.broadcasted_iota(jnp.int32, (key_block, rows), 0)
            allowed = jnp.logical_and(place >= lo_ref[...], place <= hi_ref[...])
        for g in range(per_group):
            lanes = slice(g * rows, (g + 1) * rows)
            scores = jnp.dot(keys, qt[:, lanes], preferred_element_type=jnp.float32)
            if masked:
                scores = jnp.where(allowed, scores, NEG)
            before = top[:, lanes]
            peak = jnp.maximum(before, jnp.max(scores, axis=0, keepdims=True))
            weights = jnp.exp2((scores - peak) * factor)
            shrink = jnp.exp2((before - peak) * factor)
            top[:, lanes] = peak
            total[:, lanes] = total[:, lanes] * shrink + jnp.sum(weights, axis=0, keepdims=True)
            acc[:, lanes] = acc[:, lanes] * shrink + lax.dot_general(
                values,
                weights.astype(jnp.bfloat16),
                (((0,), (0,)), ((), ())),
                preferred_element_type=jnp.float32,
            )
        return 0

    first, full_first, full_end, end = marks[0], marks[1], marks[2], marks[3]
    lax.fori_loop(first, full_first, functools.partial(step, True), 0)
    lax.fori_loop(full_first, full_end, functools.partial(step, False), 0)
    lax.fori_loop(full_end, end, functools.partial(step, True), 0)
    for g in range(per_group):
        lanes = slice(g * rows, (g + 1) * rows)
        mixed = (acc[:, lanes] / total[:, lanes]).T
        out_ref[:, g * HD : (g + 1) * HD] = mixed.astype(out_ref.dtype)


def attend(queries, window, lo, hi):
    rows = queries.shape[0]
    n_keys = window.shape[0]
    key_block = math.gcd(n_keys, 512)
    per_group = QH // KVH
    lo_min, lo_max, hi_min, hi_max = jnp.min(lo), jnp.max(lo), jnp.min(hi), jnp.max(hi)
    first = lo_min // key_block
    end = hi_max // key_block + 1
    full_first = jnp.minimum((lo_max + key_block - 1) // key_block, end)
    full_end = jnp.maximum((hi_min + 1) // key_block, full_first)
    marks = jnp.stack([first, full_first, full_end, end]).astype(jnp.int32)
    wide = per_group * HD
    return pl.pallas_call(
        functools.partial(attend_kernel, key_block),
        grid=(KVH,),
        in_specs=[
            pl.BlockSpec(memory_space=pltpu.SMEM),
            pl.BlockSpec((1, rows), lambda h: (0, 0)),
            pl.BlockSpec((1, rows), lambda h: (0, 0)),
            pl.BlockSpec((rows, wide), lambda h: (0, h)),
            pl.BlockSpec((n_keys, HD), lambda h: (0, h)),
            pl.BlockSpec((n_keys, HD), lambda h: (0, KVH + h)),
        ],
        out_specs=pl.BlockSpec((rows, wide), lambda h: (0, h)),
        out_shape=jax.ShapeDtypeStruct(queries.shape, queries.dtype),
        scratch_shapes=[
            pltpu.VMEM((HD, per_group * rows), jnp.bfloat16),
            pltpu.VMEM((1, per_group * rows), jnp.float32),
            pltpu.VMEM((1, per_group * rows), jnp.float32),
            pltpu.VMEM((HD, per_group * rows), jnp.float32),
        ],
        name="attend",
    )(marks, lo[None, :], hi[None, :], queries, window, window)


def key_range(doc_ids, rows, block_rows, seq_place, fsdp_place, modality):
    start = seq_place * block_rows + fsdp_place * rows
    here = lax.dynamic_slice_in_dim(doc_ids, start, rows, 0)
    query_pos = start + jnp.arange(rows, dtype=jnp.int32)
    below = jnp.sum((doc_ids[None, :] < here[:, None]).astype(jnp.int32), axis=1)
    upto = jnp.sum((doc_ids[None, :] <= here[:, None]).astype(jnp.int32), axis=1)
    last = jnp.minimum(upto - 1, (seq_place + 1) * block_rows - 1)
    base = (seq_place - SPAN) * block_rows
    lo = below - base
    hi = jnp.where(modality == 1, last, query_pos) - base
    return lo, hi


def flip(place, bits):
    out = place
    bit = 1
    while bit <= bits:
        if bits & bit:
            out = out + bit * (1 - 2 * (lax.div(place, bit) % 2))
        bit *= 2
    return out


def project_kernel(slices, fsdp, mod_ref, hidden_ref, w_ref, out_ref, held, acc, send, recv):
    seq_place = lax.axis_index("seq")
    fsdp_place = lax.axis_index("fsdp")
    depth = w_ref.shape[1]
    width = w_ref.shape[2] // slices
    place = seq_place % slices
    base = seq_place - place
    odd = place % 2
    near = 2 + 2 * odd
    far = 4 - 2 * odd

    def step_over(value, bit):
        return value + bit * (1 - 2 * (lax.div(value, bit) % 2))

    near_place = step_over(place, near)
    far_place = step_over(place, far)
    both_place = step_over(near_place, far)
    twin_place = flip(place, 1)
    own_places = (place, near_place, far_place, both_place)
    twin_near = flip(far_place, 1)
    twin_far = flip(near_place, 1)
    twin_places = (twin_place, twin_near, twin_far, flip(both_place, 1))

    barrier = pltpu.get_barrier_semaphore()
    greeted = [(seq_place, flip(fsdp_place, d)) for d in range(1, fsdp)]
    greeted += [(base + other, fsdp_place) for other in (near_place, far_place, twin_place)]
    for device in greeted:
        pl.semaphore_signal(barrier, inc=1, device_id=device, device_id_type=pl.DeviceIdType.MESH)
    pl.semaphore_wait(barrier, len(greeted))

    def first(d):
        return pltpu.make_async_remote_copy(
            src_ref=w_ref.at[:, :, pl.ds(pl.multiple_of(place * width, width), width)],
            dst_ref=held.at[d - 1, 0],
            send_sem=send.at[d - 1, 0],
            recv_sem=recv.at[d - 1, 0],
            device_id=(seq_place, flip(fsdp_place, d)),
            device_id_type=pl.DeviceIdType.MESH,
        )

    def onward(d, source, target, other, number):
        return pltpu.make_async_remote_copy(
            src_ref=held.at[d - 1, source],
            dst_ref=held.at[d - 1, target],
            send_sem=send.at[d - 1, number],
            recv_sem=recv.at[d - 1, target],
            device_id=(base + other, fsdp_place),
            device_id_type=pl.DeviceIdType.MESH,
        )

    def copies(d):
        return {
            "first": first(d),
            "near": onward(d, 0, 1, near_place, 1),
            "far": onward(d, 0, 2, far_place, 2),
            "both": onward(d, 1, 3, far_place, 3),
            "twin0": onward(d, 0, 4, twin_place, 4),
            "twin1": onward(d, 1, 5, twin_place, 5),
            "twin2": onward(d, 2, 6, twin_place, 6),
            "twin3": onward(d, 3, 7, twin_place, 7),
        }

    plan = {d: copies(d) for d in range(1, fsdp)}
    for d in range(1, fsdp):
        plan[d]["first"].start()

    image = mod_ref[0] == 1

    def add(d, slot, at):
        weight = jnp.where(image, held[d - 1, slot, 1], held[d - 1, slot, 0])
        rows = hidden_ref[:, pl.ds(pl.multiple_of(flip(fsdp_place, d) * depth, 128), depth)]
        acc[at] += jnp.dot(rows, weight, preferred_element_type=jnp.float32)

    own_rows = hidden_ref[:, pl.ds(pl.multiple_of(fsdp_place * depth, 128), depth)]
    for at in range(slices):
        columns = slice(at * width, (at + 1) * width)
        weight = jnp.where(image, w_ref[1, :, columns], w_ref[0, :, columns])
        acc[at] = jnp.dot(own_rows, weight, preferred_element_type=jnp.float32)

    def got_first(d):
        plan[d]["first"].wait_recv()
        plan[d]["near"].start()
        plan[d]["far"].start()
        plan[d]["twin0"].start()

    def got_near(d):
        plan[d]["near"].wait_recv()
        plan[d]["both"].start()
        plan[d]["twin1"].start()

    def got_far(d):
        plan[d]["far"].wait_recv()
        plan[d]["twin2"].start()
        plan[d]["both"].wait_recv()
        plan[d]["twin3"].start()

    def use(d):
        for slot in range(4):
            add(d, slot, own_places[slot])
        for slot in range(4):
            plan[d]["twin%d" % slot].wait_recv()
            add(d, 4 + slot, twin_places[slot])

    got_first(1)
    for d in range(1, fsdp):
        got_near(d)
        if d + 1 < fsdp:
            got_first(d + 1)
        got_far(d)
        if d > 1:
            use(d - 1)
    use(fsdp - 1)
    for at in range(slices):
        out_ref[:, at * width : (at + 1) * width] = acc[at].astype(out_ref.dtype)
    for d in range(1, fsdp):
        for copy in plan[d].values():
            copy.wait_send()


def project(hidden, kv_weights, image_groups):
    fsdp = lax.axis_size("fsdp")
    rows = hidden.shape[0]
    _, depth, kv_width = kv_weights.shape
    slices = 8
    width = kv_width // slices
    vmem = pl.BlockSpec(memory_space=pltpu.VMEM)
    return pl.pallas_call(
        functools.partial(project_kernel, slices, fsdp),
        in_specs=[pl.BlockSpec(memory_space=pltpu.SMEM), vmem, vmem],
        out_specs=vmem,
        out_shape=jax.ShapeDtypeStruct((rows, kv_width), jnp.bfloat16),
        scratch_shapes=[
            pltpu.VMEM((fsdp - 1, slices, 2, depth, width), jnp.bfloat16),
            pltpu.VMEM((slices, rows, width), jnp.float32),
            pltpu.SemaphoreType.DMA((fsdp - 1, slices)),
            pltpu.SemaphoreType.DMA((fsdp - 1, slices)),
        ],
        compiler_params=pltpu.CompilerParams(
            collective_id=0, has_side_effects=True, vmem_limit_bytes=48 * 1024 * 1024
        ),
        name="project",
    )(image_groups, hidden, kv_weights)


def local(hidden, queries, kv_weights, image_groups, doc_ids):
    rows = hidden.shape[0]
    block_rows = rows * lax.axis_size("fsdp")
    seq_place = lax.axis_index("seq")
    fsdp_place = lax.axis_index("fsdp")
    modality = image_groups[0]
    lo, hi = key_range(doc_ids, rows, block_rows, seq_place, fsdp_place, modality)
    own_kv = project(hidden, kv_weights, image_groups)
    block_kv = lax.all_gather(own_kv, "fsdp", axis=0, tiled=True)
    pieces = [from_behind(block_kv, "seq", offset) for offset in range(SPAN, 0, -1)]
    window = jnp.concatenate(pieces + [block_kv], 0)
    return attend(queries, window, lo, hi)


def solution(mesh):
    in_specs = (
        P(("seq", "fsdp"), None),
        P(("seq", "fsdp"), None),
        P(None, "fsdp", None),
        P("seq"),
        P(),
    )
    out_specs = P(("seq", "fsdp"), None)
    return jax.shard_map(local, mesh=mesh, in_specs=in_specs, out_specs=out_specs, check_vma=False)
```

```python
import functools
import math

import jax
import jax.numpy as jnp
from jax import lax
from jax.experimental import pallas as pl
from jax.experimental.pallas import tpu as pltpu
from jax.sharding import PartitionSpec as P

KVH = 4
HD = 128
QH = 16
SPAN = 3
NEG = -1e30


def attend_kernel(key_block, marks, lo_ref, hi_ref, q_ref, k_ref, v_ref, out_ref, qt, top, total, acc):
    rows = q_ref.shape[0]
    per_group = QH // KVH
    factor = math.log2(math.e) / math.sqrt(HD)
    for g in range(per_group):
        qt[:, g * rows : (g + 1) * rows] = q_ref[:, g * HD : (g + 1) * HD].T
    top[...] = jnp.full_like(top, NEG)
    total[...] = jnp.zeros_like(total)
    acc[...] = jnp.zeros_like(acc)

    def step(masked, b, _):
        at = pl.multiple_of(b * key_block, key_block)
        keys = k_ref[pl.ds(at, key_block), :]
        values = v_ref[pl.ds(at, key_block), :]
        if masked:
            place = at + lax.broadcasted_iota(jnp.int32, (key_block, rows), 0)
            allowed = jnp.logical_and(place >= lo_ref[...], place <= hi_ref[...])
        for g in range(per_group):
            lanes = slice(g * rows, (g + 1) * rows)
            scores = jnp.dot(keys, qt[:, lanes], preferred_element_type=jnp.float32)
            if masked:
                scores = jnp.where(allowed, scores, NEG)
            before = top[:, lanes]
            peak = jnp.maximum(before, jnp.max(scores, axis=0, keepdims=True))
            weights = jnp.exp2((scores - peak) * factor)
            shrink = jnp.exp2((before - peak) * factor)
            top[:, lanes] = peak
            total[:, lanes] = total[:, lanes] * shrink + jnp.sum(weights, axis=0, keepdims=True)
            acc[:, lanes] = acc[:, lanes] * shrink + lax.dot_general(
                values,
                weights.astype(jnp.bfloat16),
                (((0,), (0,)), ((), ())),
                preferred_element_type=jnp.float32,
            )
        return 0

    first, full_first, full_end, end = marks[0], marks[1], marks[2], marks[3]
    lax.fori_loop(first, full_first, functools.partial(step, True), 0)
    lax.fori_loop(full_first, full_end, functools.partial(step, False), 0)
    lax.fori_loop(full_end, end, functools.partial(step, True), 0)
    for g in range(per_group):
        lanes = slice(g * rows, (g + 1) * rows)
        mixed = (acc[:, lanes] / total[:, lanes]).T
        out_ref[:, g * HD : (g + 1) * HD] = mixed.astype(out_ref.dtype)


def attend(queries, window, lo, hi):
    rows = queries.shape[0]
    n_keys = window.shape[0]
    key_block = math.gcd(n_keys, 512)
    per_group = QH // KVH
    lo_min, lo_max, hi_min, hi_max = jnp.min(lo), jnp.max(lo), jnp.min(hi), jnp.max(hi)
    first = lo_min // key_block
    end = hi_max // key_block + 1
    full_first = jnp.minimum((lo_max + key_block - 1) // key_block, end)
    full_end = jnp.maximum((hi_min + 1) // key_block, full_first)
    marks = jnp.stack([first, full_first, full_end, end]).astype(jnp.int32)
    wide = per_group * HD
    return pl.pallas_call(
        functools.partial(attend_kernel, key_block),
        grid=(KVH,),
        in_specs=[
            pl.BlockSpec(memory_space=pltpu.SMEM),
            pl.BlockSpec((1, rows), lambda h: (0, 0)),
            pl.BlockSpec((1, rows), lambda h: (0, 0)),
            pl.BlockSpec((rows, wide), lambda h: (0, h)),
            pl.BlockSpec((n_keys, HD), lambda h: (0, h)),
            pl.BlockSpec((n_keys, HD), lambda h: (0, KVH + h)),
        ],
        out_specs=pl.BlockSpec((rows, wide), lambda h: (0, h)),
        out_shape=jax.ShapeDtypeStruct(queries.shape, queries.dtype),
        scratch_shapes=[
            pltpu.VMEM((HD, per_group * rows), jnp.bfloat16),
            pltpu.VMEM((1, per_group * rows), jnp.float32),
            pltpu.VMEM((1, per_group * rows), jnp.float32),
            pltpu.VMEM((HD, per_group * rows), jnp.float32),
        ],
        name="attend",
    )(marks, lo[None, :], hi[None, :], queries, window, window)


def key_range(doc_ids, rows, block_rows, seq_place, fsdp_place, modality):
    start = seq_place * block_rows + fsdp_place * rows
    here = lax.dynamic_slice_in_dim(doc_ids, start, rows, 0)
    query_pos = start + jnp.arange(rows, dtype=jnp.int32)
    below = jnp.sum((doc_ids[None, :] < here[:, None]).astype(jnp.int32), axis=1)
    upto = jnp.sum((doc_ids[None, :] <= here[:, None]).astype(jnp.int32), axis=1)
    last = jnp.minimum(upto - 1, (seq_place + 1) * block_rows - 1)
    base = (seq_place - SPAN) * block_rows
    lo = below - base
    hi = jnp.where(modality == 1, last, query_pos) - base
    return lo, hi


def flip(place, bits):
    out = place
    bit = 1
    while bit <= bits:
        if bits & bit:
            out = out + bit * (1 - 2 * (lax.div(place, bit) % 2))
        bit *= 2
    return out


def project_kernel(slices, fsdp, mod_ref, hidden_ref, w_ref, out_ref, held, acc, send, recv):
    seq_place = lax.axis_index("seq")
    fsdp_place = lax.axis_index("fsdp")
    depth = w_ref.shape[1]
    width = w_ref.shape[2] // slices
    place = seq_place % slices
    base = seq_place - place
    odd = place % 2
    near = 2 + 2 * odd
    far = 4 - 2 * odd

    def step_over(value, bit):
        return value + bit * (1 - 2 * (lax.div(value, bit) % 2))

    near_place = step_over(place, near)
    far_place = step_over(place, far)
    both_place = step_over(near_place, far)
    twin_place = flip(place, 1)
    own_places = (place, near_place, far_place, both_place)
    twin_near = flip(far_place, 1)
    twin_far = flip(near_place, 1)
    twin_places = (twin_place, twin_near, twin_far, flip(both_place, 1))

    barrier = pltpu.get_barrier_semaphore()
    greeted = [(seq_place, flip(fsdp_place, d)) for d in range(1, fsdp)]
    greeted += [(base + other, fsdp_place) for other in (near_place, far_place, twin_place)]
    for device in greeted:
        pl.semaphore_signal(barrier, inc=1, device_id=device, device_id_type=pl.DeviceIdType.MESH)
    pl.semaphore_wait(barrier, len(greeted))

    def first(d):
        return pltpu.make_async_remote_copy(
            src_ref=w_ref.at[:, :, pl.ds(pl.multiple_of(place * width, width), width)],
            dst_ref=held.at[d - 1, 0],
            send_sem=send.at[d - 1, 0],
            recv_sem=recv.at[d - 1, 0],
            device_id=(seq_place, flip(fsdp_place, d)),
            device_id_type=pl.DeviceIdType.MESH,
        )

    def onward(d, source, target, other, number):
        return pltpu.make_async_remote_copy(
            src_ref=held.at[d - 1, source],
            dst_ref=held.at[d - 1, target],
            send_sem=send.at[d - 1, number],
            recv_sem=recv.at[d - 1, target],
            device_id=(base + other, fsdp_place),
            device_id_type=pl.DeviceIdType.MESH,
        )

    def copies(d):
        return {
            "first": first(d),
            "near": onward(d, 0, 1, near_place, 1),
            "far": onward(d, 0, 2, far_place, 2),
            "both": onward(d, 1, 3, far_place, 3),
            "twin0": onward(d, 0, 4, twin_place, 4),
            "twin1": onward(d, 1, 5, twin_place, 5),
            "twin2": onward(d, 2, 6, twin_place, 6),
            "twin3": onward(d, 3, 7, twin_place, 7),
        }

    plan = {d: copies(d) for d in range(1, fsdp)}
    for d in range(1, fsdp):
        plan[d]["first"].start()

    image = mod_ref[0] == 1

    def add(d, slot, at):
        weight = jnp.where(image, held[d - 1, slot, 1], held[d - 1, slot, 0])
        rows = hidden_ref[:, pl.ds(pl.multiple_of(flip(fsdp_place, d) * depth, 128), depth)]
        acc[at] += jnp.dot(rows, weight, preferred_element_type=jnp.float32)

    own_rows = hidden_ref[:, pl.ds(pl.multiple_of(fsdp_place * depth, 128), depth)]
    for at in range(slices):
        columns = slice(at * width, (at + 1) * width)
        weight = jnp.where(image, w_ref[1, :, columns], w_ref[0, :, columns])
        acc[at] = jnp.dot(own_rows, weight, preferred_element_type=jnp.float32)

    def got_first(d):
        plan[d]["first"].wait_recv()
        plan[d]["near"].start()
        plan[d]["far"].start()
        plan[d]["twin0"].start()

    def got_near(d):
        plan[d]["near"].wait_recv()
        plan[d]["both"].start()
        plan[d]["twin1"].start()

    def got_far(d):
        plan[d]["far"].wait_recv()
        plan[d]["twin2"].start()
        plan[d]["both"].wait_recv()
        plan[d]["twin3"].start()

    def use(d):
        for slot in range(4):
            add(d, slot, own_places[slot])
        for slot in range(4):
            plan[d]["twin%d" % slot].wait_recv()
            add(d, 4 + slot, twin_places[slot])

    got_first(1)
    for d in range(1, fsdp):
        got_near(d)
        if d + 1 < fsdp:
            got_first(d + 1)
        got_far(d)
        if d > 1:
            use(d - 1)
    use(fsdp - 1)
    for at in range(slices):
        out_ref[:, at * width : (at + 1) * width] = acc[at].astype(out_ref.dtype)
    for d in range(1, fsdp):
        for copy in plan[d].values():
            copy.wait_send()


def project(hidden, kv_weights, image_groups):
    fsdp = lax.axis_size("fsdp")
    rows = hidden.shape[0]
    _, depth, kv_width = kv_weights.shape
    slices = 8
    width = kv_width // slices
    vmem = pl.BlockSpec(memory_space=pltpu.VMEM)
    return pl.pallas_call(
        functools.partial(project_kernel, slices, fsdp),
        in_specs=[pl.BlockSpec(memory_space=pltpu.SMEM), vmem, vmem],
        out_specs=vmem,
        out_shape=jax.ShapeDtypeStruct((rows, kv_width), jnp.bfloat16),
        scratch_shapes=[
            pltpu.VMEM((fsdp - 1, slices, 2, depth, width), jnp.bfloat16),
            pltpu.VMEM((slices, rows, width), jnp.float32),
            pltpu.SemaphoreType.DMA((fsdp - 1, slices)),
            pltpu.SemaphoreType.DMA((fsdp - 1, slices)),
        ],
        compiler_params=pltpu.CompilerParams(
            collective_id=0, has_side_effects=True, vmem_limit_bytes=48 * 1024 * 1024
        ),
        name="project",
    )(image_groups, hidden, kv_weights)


def collect_kernel(seq, fsdp, own_ref, out_ref, send, recv, local_sem):
    s = lax.axis_index("seq")
    z = lax.axis_index("fsdp")
    odd = s % 2
    pair_odd = lax.div(s, 2) % 2

    barrier = pltpu.get_barrier_semaphore()
    greeted = [(s, flip(z, d)) for d in range(1, fsdp)]
    greeted += [((s + o + seq) % seq, z) for o in range(-SPAN, SPAN + 1) if o]
    for device in greeted:
        pl.semaphore_signal(barrier, inc=1, device_id=device, device_id_type=pl.DeviceIdType.MESH)
    pl.semaphore_wait(barrier, len(greeted))

    def held(back, d):
        return out_ref.at[SPAN - back, flip(z, d)]

    def own(d):
        return own_ref if d == 0 else held(0, d)

    def copy(source, back, d, number, ahead):
        return pltpu.make_async_remote_copy(
            src_ref=source,
            dst_ref=held(back, d),
            send_sem=send.at[number, d],
            recv_sem=recv.at[back, d],
            device_id=((s + ahead + seq) % seq, z),
            device_id_type=pl.DeviceIdType.MESH,
        )

    def across(d):
        return pltpu.make_async_remote_copy(
            src_ref=own_ref,
            dst_ref=held(0, 0),
            send_sem=send.at[0, d],
            recv_sem=recv.at[0, d],
            device_id=(s, flip(z, d)),
            device_id_type=pl.DeviceIdType.MESH,
        )

    even = odd == 0
    uneven = odd == 1
    both = jnp.logical_and
    sends = [
        (both(even, s + 2 < seq), lambda d: copy(own(d), 2, d, 1, 2)),
        (even, lambda d: copy(own(d), 1, d, 2, 1)),
        (both(uneven, both(pair_odd == 0, s + 2 < seq)), lambda d: copy(own(d), 2, d, 1, 2)),
        (both(uneven, s + 3 < seq), lambda d: copy(own(d), 3, d, 2, 3)),
    ]
    after_two = [
        (both(even, s >= 2), lambda d: copy(held(2, d), 3, d, 3, 1)),
        (both(uneven, s >= 2), lambda d: copy(held(2, d), 1, d, 3, -1)),
    ]
    after_three = [(both(even, both(pair_odd == 1, s >= 4)), lambda d: copy(held(3, d), 2, d, 4, -1))]
    got_two = s >= 2
    got_three_early = both(even, s >= 4)
    got_three_late = both(uneven, s >= 3)
    got_one = jnp.logical_or(uneven, s >= 2)

    def each(items, d, act):
        for holds, make in items:
            @pl.when(holds)
            def _(make=make):
                act(make(d))

    def start(items, d):
        each(items, d, lambda c: c.start())

    def arrived(holds, back, d):
        @pl.when(holds)
        def _():
            copy(own_ref, back, d, 1, 1).wait_recv()

    keep = pltpu.make_async_copy(own_ref, held(0, 0), local_sem)
    keep.start()
    for d in range(1, fsdp):
        across(d).start()
    start(sends, 0)

    def relay(d):
        arrived(got_three_early, 3, d)
        start(after_three, d)
        arrived(got_two, 2, d)
        start(after_two, d)

    for d in range(1, fsdp):
        across(d).wait_recv()
        start(sends, d)
        relay(d - 1)
    relay(fsdp - 1)
    for d in range(fsdp):
        arrived(got_three_late, 3, d)
        arrived(got_one, 1, d)
    keep.wait()
    for d in range(fsdp):
        if d:
            across(d).wait_send()
        each(sends + after_two + after_three, d, lambda c: c.wait_send())


def collect(own_kv):
    seq, fsdp = lax.axis_size("seq"), lax.axis_size("fsdp")
    rows, width = own_kv.shape
    anywhere = pl.BlockSpec(memory_space=pl.ANY)
    window = pl.pallas_call(
        functools.partial(collect_kernel, seq, fsdp),
        in_specs=[pl.BlockSpec(memory_space=pltpu.VMEM)],
        out_specs=anywhere,
        out_shape=jax.ShapeDtypeStruct((SPAN + 1, fsdp, rows, width), own_kv.dtype),
        scratch_shapes=[
            pltpu.SemaphoreType.DMA((5, fsdp)),
            pltpu.SemaphoreType.DMA((SPAN + 1, fsdp)),
            pltpu.SemaphoreType.DMA,
        ],
        compiler_params=pltpu.CompilerParams(collective_id=1, has_side_effects=True),
        name="collect",
    )(own_kv)
    return window.reshape((SPAN + 1) * fsdp * rows, width)


def local(hidden, queries, kv_weights, image_groups, doc_ids):
    rows = hidden.shape[0]
    block_rows = rows * lax.axis_size("fsdp")
    seq_place = lax.axis_index("seq")
    fsdp_place = lax.axis_index("fsdp")
    modality = image_groups[0]
    lo, hi = key_range(doc_ids, rows, block_rows, seq_place, fsdp_place, modality)
    own_kv = project(hidden, kv_weights, image_groups)
    window = collect(own_kv)
    return attend(queries, window, lo, hi)


def solution(mesh):
    in_specs = (
        P(("seq", "fsdp"), None),
        P(("seq", "fsdp"), None),
        P(None, "fsdp", None),
        P("seq"),
        P(),
    )
    out_specs = P(("seq", "fsdp"), None)
    return jax.shard_map(local, mesh=mesh, in_specs=in_specs, out_specs=out_specs, check_vma=False)
```

```python
import functools
import math

import jax
import jax.numpy as jnp
from jax import lax
from jax.experimental import pallas as pl
from jax.experimental.pallas import tpu as pltpu
from jax.sharding import PartitionSpec as P

KVH = 4
HD = 128
QH = 16
SPAN = 3
NEG = -1e30


def attend_kernel(key_block, marks, lo_ref, hi_ref, q_ref, k_ref, v_ref, out_ref, qt, top, total, acc):
    rows = q_ref.shape[0]
    per_group = QH // KVH
    lanes = [slice(g * rows, (g + 1) * rows) for g in range(per_group)]
    factor = math.log2(math.e) / math.sqrt(HD)
    for g in range(per_group):
        qt[:, g * rows : (g + 1) * rows] = q_ref[:, g * HD : (g + 1) * HD].T
    top[...] = jnp.full_like(top, NEG)
    total[...] = jnp.zeros_like(total)
    acc[...] = jnp.zeros_like(acc)

    def step(masked, b, _):
        at = pl.multiple_of(b * key_block, key_block)
        keys = k_ref[pl.ds(at, key_block), :]
        values = v_ref[pl.ds(at, key_block), :]
        if masked:
            place = at + lax.broadcasted_iota(jnp.int32, (key_block, rows), 0)
            allowed = jnp.logical_and(place >= lo_ref[...], place <= hi_ref[...])
        scores = [jnp.dot(keys, qt[:, at_g], preferred_element_type=jnp.float32) for at_g in lanes]
        if masked:
            scores = [jnp.where(allowed, score, NEG) for score in scores]
        before = [top[:, at_g] for at_g in lanes]
        peak = [
            jnp.maximum(old, jnp.max(score, axis=0, keepdims=True))
            for old, score in zip(before, scores)
        ]
        weights = [jnp.exp2((score - high) * factor) for score, high in zip(scores, peak)]
        shrink = [jnp.exp2((old - high) * factor) for old, high in zip(before, peak)]
        added = [jnp.sum(weight, axis=0, keepdims=True) for weight in weights]
        mixed = [
            lax.dot_general(
                values,
                weight.astype(jnp.bfloat16),
                (((0,), (0,)), ((), ())),
                preferred_element_type=jnp.float32,
            )
            for weight in weights
        ]
        for g, at_g in enumerate(lanes):
            top[:, at_g] = peak[g]
            total[:, at_g] = total[:, at_g] * shrink[g] + added[g]
            acc[:, at_g] = acc[:, at_g] * shrink[g] + mixed[g]
        return 0

    first, full_first, full_end, end = marks[0], marks[1], marks[2], marks[3]
    lax.fori_loop(first, full_first, functools.partial(step, True), 0)
    lax.fori_loop(full_first, full_end, functools.partial(step, False), 0)
    lax.fori_loop(full_end, end, functools.partial(step, True), 0)
    for g in range(per_group):
        mixed = (acc[:, lanes[g]] / total[:, lanes[g]]).T
        out_ref[:, g * HD : (g + 1) * HD] = mixed.astype(out_ref.dtype)


def attend(queries, window, lo, hi):
    rows = queries.shape[0]
    n_keys = window.shape[0]
    key_block = math.gcd(n_keys, 512)
    per_group = QH // KVH
    lo_min, lo_max, hi_min, hi_max = jnp.min(lo), jnp.max(lo), jnp.min(hi), jnp.max(hi)
    first = lo_min // key_block
    end = hi_max // key_block + 1
    full_first = jnp.minimum((lo_max + key_block - 1) // key_block, end)
    full_end = jnp.maximum((hi_min + 1) // key_block, full_first)
    marks = jnp.stack([first, full_first, full_end, end]).astype(jnp.int32)
    wide = per_group * HD
    return pl.pallas_call(
        functools.partial(attend_kernel, key_block),
        grid=(KVH,),
        in_specs=[
            pl.BlockSpec(memory_space=pltpu.SMEM),
            pl.BlockSpec((1, rows), lambda h: (0, 0)),
            pl.BlockSpec((1, rows), lambda h: (0, 0)),
            pl.BlockSpec((rows, wide), lambda h: (0, h)),
            pl.BlockSpec((n_keys, HD), lambda h: (0, h)),
            pl.BlockSpec((n_keys, HD), lambda h: (0, KVH + h)),
        ],
        out_specs=pl.BlockSpec((rows, wide), lambda h: (0, h)),
        out_shape=jax.ShapeDtypeStruct(queries.shape, queries.dtype),
        scratch_shapes=[
            pltpu.VMEM((HD, per_group * rows), jnp.bfloat16),
            pltpu.VMEM((1, per_group * rows), jnp.float32),
            pltpu.VMEM((1, per_group * rows), jnp.float32),
            pltpu.VMEM((HD, per_group * rows), jnp.float32),
        ],
        name="attend",
    )(marks, lo[None, :], hi[None, :], queries, window, window)


def key_range(doc_ids, rows, block_rows, seq_place, fsdp_place, modality):
    start = seq_place * block_rows + fsdp_place * rows
    here = lax.dynamic_slice_in_dim(doc_ids, start, rows, 0)
    query_pos = start + jnp.arange(rows, dtype=jnp.int32)
    below = jnp.sum((doc_ids[None, :] < here[:, None]).astype(jnp.int32), axis=1)
    upto = jnp.sum((doc_ids[None, :] <= here[:, None]).astype(jnp.int32), axis=1)
    last = jnp.minimum(upto - 1, (seq_place + 1) * block_rows - 1)
    base = (seq_place - SPAN) * block_rows
    lo = below - base
    hi = jnp.where(modality == 1, last, query_pos) - base
    return lo, hi


def flip(place, bits):
    out = place
    bit = 1
    while bit <= bits:
        if bits & bit:
            out = out + bit * (1 - 2 * (lax.div(place, bit) % 2))
        bit *= 2
    return out


def project_kernel(slices, fsdp, mod_ref, hidden_ref, w_ref, out_ref, held, acc, send, recv):
    seq_place = lax.axis_index("seq")
    fsdp_place = lax.axis_index("fsdp")
    depth = w_ref.shape[1]
    width = w_ref.shape[2] // slices
    place = seq_place % slices
    base = seq_place - place
    odd = place % 2
    near = 2 + 2 * odd
    far = 4 - 2 * odd

    def step_over(value, bit):
        return value + bit * (1 - 2 * (lax.div(value, bit) % 2))

    near_place = step_over(place, near)
    far_place = step_over(place, far)
    both_place = step_over(near_place, far)
    twin_place = flip(place, 1)
    own_places = (place, near_place, far_place, both_place)
    twin_near = flip(far_place, 1)
    twin_far = flip(near_place, 1)
    twin_places = (twin_place, twin_near, twin_far, flip(both_place, 1))

    barrier = pltpu.get_barrier_semaphore()
    greeted = [(seq_place, flip(fsdp_place, d)) for d in range(1, fsdp)]
    greeted += [(base + other, fsdp_place) for other in (near_place, far_place, twin_place)]
    for device in greeted:
        pl.semaphore_signal(barrier, inc=1, device_id=device, device_id_type=pl.DeviceIdType.MESH)
    pl.semaphore_wait(barrier, len(greeted))

    def first(d):
        return pltpu.make_async_remote_copy(
            src_ref=w_ref.at[:, :, pl.ds(pl.multiple_of(place * width, width), width)],
            dst_ref=held.at[d - 1, 0],
            send_sem=send.at[d - 1, 0],
            recv_sem=recv.at[d - 1, 0],
            device_id=(seq_place, flip(fsdp_place, d)),
            device_id_type=pl.DeviceIdType.MESH,
        )

    def onward(d, source, target, other, number):
        return pltpu.make_async_remote_copy(
            src_ref=held.at[d - 1, source],
            dst_ref=held.at[d - 1, target],
            send_sem=send.at[d - 1, number],
            recv_sem=recv.at[d - 1, target],
            device_id=(base + other, fsdp_place),
            device_id_type=pl.DeviceIdType.MESH,
        )

    def copies(d):
        return {
            "first": first(d),
            "near": onward(d, 0, 1, near_place, 1),
            "far": onward(d, 0, 2, far_place, 2),
            "both": onward(d, 1, 3, far_place, 3),
            "twin0": onward(d, 0, 4, twin_place, 4),
            "twin1": onward(d, 1, 5, twin_place, 5),
            "twin2": onward(d, 2, 6, twin_place, 6),
            "twin3": onward(d, 3, 7, twin_place, 7),
        }

    plan = {d: copies(d) for d in range(1, fsdp)}
    for d in range(1, fsdp):
        plan[d]["first"].start()

    image = mod_ref[0] == 1

    def add(d, slot, at):
        weight = jnp.where(image, held[d - 1, slot, 1], held[d - 1, slot, 0])
        rows = hidden_ref[:, pl.ds(pl.multiple_of(flip(fsdp_place, d) * depth, 128), depth)]
        acc[at] += jnp.dot(rows, weight, preferred_element_type=jnp.float32)

    own_rows = hidden_ref[:, pl.ds(pl.multiple_of(fsdp_place * depth, 128), depth)]
    for at in range(slices):
        columns = slice(at * width, (at + 1) * width)
        weight = jnp.where(image, w_ref[1, :, columns], w_ref[0, :, columns])
        acc[at] = jnp.dot(own_rows, weight, preferred_element_type=jnp.float32)

    def got_first(d):
        plan[d]["first"].wait_recv()
        plan[d]["near"].start()
        plan[d]["far"].start()
        plan[d]["twin0"].start()

    def got_near(d):
        plan[d]["near"].wait_recv()
        plan[d]["both"].start()
        plan[d]["twin1"].start()

    def got_far(d):
        plan[d]["far"].wait_recv()
        plan[d]["twin2"].start()
        plan[d]["both"].wait_recv()
        plan[d]["twin3"].start()

    def use(d):
        for slot in range(4):
            add(d, slot, own_places[slot])
        for slot in range(4):
            plan[d]["twin%d" % slot].wait_recv()
            add(d, 4 + slot, twin_places[slot])

    got_first(1)
    for d in range(1, fsdp):
        got_near(d)
        if d + 1 < fsdp:
            got_first(d + 1)
        got_far(d)
        if d > 1:
            use(d - 1)
    use(fsdp - 1)
    for at in range(slices):
        out_ref[:, at * width : (at + 1) * width] = acc[at].astype(out_ref.dtype)
    for d in range(1, fsdp):
        for copy in plan[d].values():
            copy.wait_send()


def project(hidden, kv_weights, image_groups):
    fsdp = lax.axis_size("fsdp")
    rows = hidden.shape[0]
    _, depth, kv_width = kv_weights.shape
    slices = 8
    width = kv_width // slices
    vmem = pl.BlockSpec(memory_space=pltpu.VMEM)
    return pl.pallas_call(
        functools.partial(project_kernel, slices, fsdp),
        in_specs=[pl.BlockSpec(memory_space=pltpu.SMEM), vmem, vmem],
        out_specs=vmem,
        out_shape=jax.ShapeDtypeStruct((rows, kv_width), jnp.bfloat16),
        scratch_shapes=[
            pltpu.VMEM((fsdp - 1, slices, 2, depth, width), jnp.bfloat16),
            pltpu.VMEM((slices, rows, width), jnp.float32),
            pltpu.SemaphoreType.DMA((fsdp - 1, slices)),
            pltpu.SemaphoreType.DMA((fsdp - 1, slices)),
        ],
        compiler_params=pltpu.CompilerParams(
            collective_id=0, has_side_effects=True, vmem_limit_bytes=48 * 1024 * 1024
        ),
        name="project",
    )(image_groups, hidden, kv_weights)


def collect_kernel(seq, fsdp, own_ref, out_ref, send, recv, local_sem):
    s = lax.axis_index("seq")
    z = lax.axis_index("fsdp")
    odd = s % 2
    pair_odd = lax.div(s, 2) % 2

    barrier = pltpu.get_barrier_semaphore()
    greeted = [(s, flip(z, d)) for d in range(1, fsdp)]
    greeted += [((s + o + seq) % seq, z) for o in range(-SPAN, SPAN + 1) if o]
    for device in greeted:
        pl.semaphore_signal(barrier, inc=1, device_id=device, device_id_type=pl.DeviceIdType.MESH)
    pl.semaphore_wait(barrier, len(greeted))

    def held(back, d):
        return out_ref.at[SPAN - back, flip(z, d)]

    def own(d):
        return own_ref if d == 0 else held(0, d)

    def copy(source, back, d, number, ahead):
        return pltpu.make_async_remote_copy(
            src_ref=source,
            dst_ref=held(back, d),
            send_sem=send.at[number, d],
            recv_sem=recv.at[back, d],
            device_id=((s + ahead + seq) % seq, z),
            device_id_type=pl.DeviceIdType.MESH,
        )

    def across(d):
        return pltpu.make_async_remote_copy(
            src_ref=own_ref,
            dst_ref=held(0, 0),
            send_sem=send.at[0, d],
            recv_sem=recv.at[0, d],
            device_id=(s, flip(z, d)),
            device_id_type=pl.DeviceIdType.MESH,
        )

    even = odd == 0
    uneven = odd == 1
    both = jnp.logical_and
    sends = [
        (both(even, s + 2 < seq), lambda d: copy(own(d), 2, d, 1, 2)),
        (even, lambda d: copy(own(d), 1, d, 2, 1)),
        (both(uneven, both(pair_odd == 0, s + 2 < seq)), lambda d: copy(own(d), 2, d, 1, 2)),
        (both(uneven, s + 3 < seq), lambda d: copy(own(d), 3, d, 2, 3)),
    ]
    after_two = [
        (both(even, s >= 2), lambda d: copy(held(2, d), 3, d, 3, 1)),
        (both(uneven, s >= 2), lambda d: copy(held(2, d), 1, d, 3, -1)),
    ]
    after_three = [(both(even, both(pair_odd == 1, s >= 4)), lambda d: copy(held(3, d), 2, d, 4, -1))]
    got_two = s >= 2
    got_three_early = both(even, s >= 4)
    got_three_late = both(uneven, s >= 3)
    got_one = jnp.logical_or(uneven, s >= 2)

    def each(items, d, act):
        for holds, make in items:
            @pl.when(holds)
            def _(make=make):
                act(make(d))

    def start(items, d):
        each(items, d, lambda c: c.start())

    def arrived(holds, back, d):
        @pl.when(holds)
        def _():
            copy(own_ref, back, d, 1, 1).wait_recv()

    keep = pltpu.make_async_copy(own_ref, held(0, 0), local_sem)
    keep.start()
    for d in range(1, fsdp):
        across(d).start()
    start(sends, 0)

    def relay(d):
        arrived(got_three_early, 3, d)
        start(after_three, d)
        arrived(got_two, 2, d)
        start(after_two, d)

    for d in range(1, fsdp):
        across(d).wait_recv()
        start(sends, d)
        relay(d - 1)
    relay(fsdp - 1)
    for d in range(fsdp):
        arrived(got_three_late, 3, d)
        arrived(got_one, 1, d)
    keep.wait()
    for d in range(fsdp):
        if d:
            across(d).wait_send()
        each(sends + after_two + after_three, d, lambda c: c.wait_send())


def collect(own_kv):
    seq, fsdp = lax.axis_size("seq"), lax.axis_size("fsdp")
    rows, width = own_kv.shape
    anywhere = pl.BlockSpec(memory_space=pl.ANY)
    window = pl.pallas_call(
        functools.partial(collect_kernel, seq, fsdp),
        in_specs=[pl.BlockSpec(memory_space=pltpu.VMEM)],
        out_specs=anywhere,
        out_shape=jax.ShapeDtypeStruct((SPAN + 1, fsdp, rows, width), own_kv.dtype),
        scratch_shapes=[
            pltpu.SemaphoreType.DMA((5, fsdp)),
            pltpu.SemaphoreType.DMA((SPAN + 1, fsdp)),
            pltpu.SemaphoreType.DMA,
        ],
        compiler_params=pltpu.CompilerParams(collective_id=1, has_side_effects=True),
        name="collect",
    )(own_kv)
    return window.reshape((SPAN + 1) * fsdp * rows, width)


def local(hidden, queries, kv_weights, image_groups, doc_ids):
    rows = hidden.shape[0]
    block_rows = rows * lax.axis_size("fsdp")
    seq_place = lax.axis_index("seq")
    fsdp_place = lax.axis_index("fsdp")
    modality = image_groups[0]
    lo, hi = key_range(doc_ids, rows, block_rows, seq_place, fsdp_place, modality)
    own_kv = project(hidden, kv_weights, image_groups)
    window = collect(own_kv)
    return attend(queries, window, lo, hi)


def solution(mesh):
    in_specs = (
        P(("seq", "fsdp"), None),
        P(("seq", "fsdp"), None),
        P(None, "fsdp", None),
        P("seq"),
        P(),
    )
    out_specs = P(("seq", "fsdp"), None)
    return jax.shard_map(local, mesh=mesh, in_specs=in_specs, out_specs=out_specs, check_vma=False)
```

```python
import functools
import math

import jax
import jax.numpy as jnp
from jax import lax
from jax.experimental import pallas as pl
from jax.experimental.pallas import tpu as pltpu
from jax.sharding import PartitionSpec as P

KVH = 4
HD = 128
QH = 16
SPAN = 3
NEG = -1e30


def attend_kernel(key_block, marks, lo_ref, hi_ref, q_ref, k_ref, v_ref, out_ref, qt, top, total, acc):
    rows = q_ref.shape[0]
    per_group = QH // KVH
    lanes = [slice(g * rows, (g + 1) * rows) for g in range(per_group)]
    factor = math.log2(math.e) / math.sqrt(HD)
    for g in range(per_group):
        qt[:, g * rows : (g + 1) * rows] = q_ref[:, g * HD : (g + 1) * HD].T
    top[...] = jnp.full_like(top, NEG)
    total[...] = jnp.zeros_like(total)
    acc[...] = jnp.zeros_like(acc)

    def step(masked, b, _):
        at = pl.multiple_of(b * key_block, key_block)
        keys = k_ref[pl.ds(at, key_block), :]
        values = v_ref[pl.ds(at, key_block), :]
        if masked:
            place = at + lax.broadcasted_iota(jnp.int32, (key_block, rows), 0)
            allowed = jnp.logical_and(place >= lo_ref[...], place <= hi_ref[...])
        scores = [jnp.dot(keys, qt[:, at_g], preferred_element_type=jnp.float32) for at_g in lanes]
        if masked:
            scores = [jnp.where(allowed, score, NEG) for score in scores]
        before = [top[:, at_g] for at_g in lanes]
        peak = [
            jnp.maximum(old, jnp.max(score, axis=0, keepdims=True))
            for old, score in zip(before, scores)
        ]
        weights = [jnp.exp2((score - high) * factor) for score, high in zip(scores, peak)]
        shrink = [jnp.exp2((old - high) * factor) for old, high in zip(before, peak)]
        added = [jnp.sum(weight, axis=0, keepdims=True) for weight in weights]
        mixed = [
            lax.dot_general(
                values,
                weight.astype(jnp.bfloat16),
                (((0,), (0,)), ((), ())),
                preferred_element_type=jnp.float32,
            )
            for weight in weights
        ]
        for g, at_g in enumerate(lanes):
            top[:, at_g] = peak[g]
            total[:, at_g] = total[:, at_g] * shrink[g] + added[g]
            acc[:, at_g] = acc[:, at_g] * shrink[g] + mixed[g]
        return 0

    first, full_first, full_end, end = marks[0], marks[1], marks[2], marks[3]
    lax.fori_loop(first, full_first, functools.partial(step, True), 0)
    lax.fori_loop(full_first, full_end, functools.partial(step, False), 0)
    lax.fori_loop(full_end, end, functools.partial(step, True), 0)
    for g in range(per_group):
        mixed = (acc[:, lanes[g]] / total[:, lanes[g]]).T
        out_ref[:, g * HD : (g + 1) * HD] = mixed.astype(out_ref.dtype)


def attend(queries, window, lo, hi):
    rows = queries.shape[0]
    n_keys = window.shape[0]
    key_block = math.gcd(n_keys, 512)
    per_group = QH // KVH
    lo_min, lo_max, hi_min, hi_max = jnp.min(lo), jnp.max(lo), jnp.min(hi), jnp.max(hi)
    first = lo_min // key_block
    end = hi_max // key_block + 1
    full_first = jnp.minimum((lo_max + key_block - 1) // key_block, end)
    full_end = jnp.maximum((hi_min + 1) // key_block, full_first)
    marks = jnp.stack([first, full_first, full_end, end]).astype(jnp.int32)
    wide = per_group * HD
    return pl.pallas_call(
        functools.partial(attend_kernel, key_block),
        grid=(KVH,),
        in_specs=[
            pl.BlockSpec(memory_space=pltpu.SMEM),
            pl.BlockSpec((1, rows), lambda h: (0, 0)),
            pl.BlockSpec((1, rows), lambda h: (0, 0)),
            pl.BlockSpec((rows, wide), lambda h: (0, h)),
            pl.BlockSpec((n_keys, HD), lambda h: (0, h)),
            pl.BlockSpec((n_keys, HD), lambda h: (0, KVH + h)),
        ],
        out_specs=pl.BlockSpec((rows, wide), lambda h: (0, h)),
        out_shape=jax.ShapeDtypeStruct(queries.shape, queries.dtype),
        scratch_shapes=[
            pltpu.VMEM((HD, per_group * rows), jnp.bfloat16),
            pltpu.VMEM((1, per_group * rows), jnp.float32),
            pltpu.VMEM((1, per_group * rows), jnp.float32),
            pltpu.VMEM((HD, per_group * rows), jnp.float32),
        ],
        name="attend",
    )(marks, lo[None, :], hi[None, :], queries, window, window)


def key_range(doc_ids, rows, block_rows, seq_place, fsdp_place, modality):
    start = seq_place * block_rows + fsdp_place * rows
    here = lax.dynamic_slice_in_dim(doc_ids, start, rows, 0)
    query_pos = start + jnp.arange(rows, dtype=jnp.int32)
    below = jnp.sum((doc_ids[None, :] < here[:, None]).astype(jnp.int32), axis=1)
    upto = jnp.sum((doc_ids[None, :] <= here[:, None]).astype(jnp.int32), axis=1)
    last = jnp.minimum(upto - 1, (seq_place + 1) * block_rows - 1)
    base = (seq_place - SPAN) * block_rows
    lo = below - base
    hi = jnp.where(modality == 1, last, query_pos) - base
    return lo, hi


def flip(place, bits):
    out = place
    bit = 1
    while bit <= bits:
        if bits & bit:
            out = out + bit * (1 - 2 * (lax.div(place, bit) % 2))
        bit *= 2
    return out


def project_kernel(slices, fsdp, mod_ref, hidden_ref, w_ref, out_ref, held, acc, send, recv):
    seq_place = lax.axis_index("seq")
    fsdp_place = lax.axis_index("fsdp")
    depth = w_ref.shape[1]
    width = w_ref.shape[2] // slices
    place = seq_place % slices
    base = seq_place - place
    odd = place % 2
    near = 2 + 2 * odd
    far = 4 - 2 * odd

    def step_over(value, bit):
        return value + bit * (1 - 2 * (lax.div(value, bit) % 2))

    near_place = step_over(place, near)
    far_place = step_over(place, far)
    both_place = step_over(near_place, far)
    twin_place = flip(place, 1)
    own_places = (place, near_place, far_place, both_place)
    twin_near = flip(far_place, 1)
    twin_far = flip(near_place, 1)
    twin_places = (twin_place, twin_near, twin_far, flip(both_place, 1))

    barrier = pltpu.get_barrier_semaphore()
    greeted = [(seq_place, flip(fsdp_place, d)) for d in range(1, fsdp)]
    greeted += [(base + other, fsdp_place) for other in (near_place, far_place, twin_place)]
    for device in greeted:
        pl.semaphore_signal(barrier, inc=1, device_id=device, device_id_type=pl.DeviceIdType.MESH)
    pl.semaphore_wait(barrier, len(greeted))

    def first(e):
        return pltpu.make_async_remote_copy(
            src_ref=w_ref.at[e % 2, :, pl.ds(pl.multiple_of(place * width, width), width)],
            dst_ref=held.at[e // 2, 0, e % 2],
            send_sem=send.at[e, 0],
            recv_sem=recv.at[e, 0],
            device_id=(seq_place, flip(fsdp_place, 1 + e // 2)),
            device_id_type=pl.DeviceIdType.MESH,
        )

    def onward(e, source, target, other, number):
        return pltpu.make_async_remote_copy(
            src_ref=held.at[e // 2, source, e % 2],
            dst_ref=held.at[e // 2, target, e % 2],
            send_sem=send.at[e, number],
            recv_sem=recv.at[e, target],
            device_id=(base + other, fsdp_place),
            device_id_type=pl.DeviceIdType.MESH,
        )

    def copies(e):
        return {
            "first": first(e),
            "near": onward(e, 0, 1, near_place, 1),
            "far": onward(e, 0, 2, far_place, 2),
            "both": onward(e, 1, 3, far_place, 3),
            "twin0": onward(e, 0, 4, twin_place, 4),
            "twin1": onward(e, 1, 5, twin_place, 5),
            "twin2": onward(e, 2, 6, twin_place, 6),
            "twin3": onward(e, 3, 7, twin_place, 7),
        }

    chunks = range(2 * (fsdp - 1))
    plan = {e: copies(e) for e in chunks}
    for e in chunks:
        plan[e]["first"].start()

    image = mod_ref[0] == 1

    def add(d, slot, at):
        weight = jnp.where(image, held[d - 1, slot, 1], held[d - 1, slot, 0])
        rows = hidden_ref[:, pl.ds(pl.multiple_of(flip(fsdp_place, d) * depth, 128), depth)]
        acc[at] += jnp.dot(rows, weight, preferred_element_type=jnp.float32)

    own_rows = hidden_ref[:, pl.ds(pl.multiple_of(fsdp_place * depth, 128), depth)]
    for at in range(slices):
        columns = slice(at * width, (at + 1) * width)
        weight = jnp.where(image, w_ref[1, :, columns], w_ref[0, :, columns])
        acc[at] = jnp.dot(own_rows, weight, preferred_element_type=jnp.float32)

    def got_first(d):
        plan[d]["first"].wait_recv()
        plan[d]["near"].start()
        plan[d]["far"].start()
        plan[d]["twin0"].start()

    def got_near(d):
        plan[d]["near"].wait_recv()
        plan[d]["both"].start()
        plan[d]["twin1"].start()

    def got_far(d):
        plan[d]["far"].wait_recv()
        plan[d]["twin2"].start()
        plan[d]["both"].wait_recv()
        plan[d]["twin3"].start()

    def use(d):
        for slot in range(4):
            add(d, slot, own_places[slot])
        for slot in range(4):
            for e in (2 * d - 2, 2 * d - 1):
                plan[e]["twin%d" % slot].wait_recv()
            add(d, 4 + slot, twin_places[slot])

    got_first(0)
    for e in chunks:
        got_near(e)
        if e + 1 < len(chunks):
            got_first(e + 1)
        got_far(e)
        if e % 2 and e > 1:
            use(e // 2)
    use(fsdp - 1)
    for at in range(slices):
        out_ref[:, at * width : (at + 1) * width] = acc[at].astype(out_ref.dtype)
    for e in chunks:
        for copy in plan[e].values():
            copy.wait_send()


def project(hidden, kv_weights, image_groups):
    fsdp = lax.axis_size("fsdp")
    rows = hidden.shape[0]
    _, depth, kv_width = kv_weights.shape
    slices = 8
    width = kv_width // slices
    vmem = pl.BlockSpec(memory_space=pltpu.VMEM)
    return pl.pallas_call(
        functools.partial(project_kernel, slices, fsdp),
        in_specs=[pl.BlockSpec(memory_space=pltpu.SMEM), vmem, vmem],
        out_specs=vmem,
        out_shape=jax.ShapeDtypeStruct((rows, kv_width), jnp.bfloat16),
        scratch_shapes=[
            pltpu.VMEM((fsdp - 1, slices, 2, depth, width), jnp.bfloat16),
            pltpu.VMEM((slices, rows, width), jnp.float32),
            pltpu.SemaphoreType.DMA((2 * fsdp - 2, slices)),
            pltpu.SemaphoreType.DMA((2 * fsdp - 2, slices)),
        ],
        compiler_params=pltpu.CompilerParams(
            collective_id=0, has_side_effects=True, vmem_limit_bytes=48 * 1024 * 1024
        ),
        name="project",
    )(image_groups, hidden, kv_weights)


def collect_kernel(seq, fsdp, own_ref, out_ref, send, recv, local_sem):
    s = lax.axis_index("seq")
    z = lax.axis_index("fsdp")
    odd = s % 2
    pair_odd = lax.div(s, 2) % 2

    barrier = pltpu.get_barrier_semaphore()
    greeted = [(s, flip(z, d)) for d in range(1, fsdp)]
    greeted += [((s + o + seq) % seq, z) for o in range(-SPAN, SPAN + 1) if o]
    for device in greeted:
        pl.semaphore_signal(barrier, inc=1, device_id=device, device_id_type=pl.DeviceIdType.MESH)
    pl.semaphore_wait(barrier, len(greeted))

    def held(back, d):
        return out_ref.at[SPAN - back, flip(z, d)]

    def own(d):
        return own_ref if d == 0 else held(0, d)

    def copy(source, back, d, number, ahead):
        return pltpu.make_async_remote_copy(
            src_ref=source,
            dst_ref=held(back, d),
            send_sem=send.at[number, d],
            recv_sem=recv.at[back, d],
            device_id=((s + ahead + seq) % seq, z),
            device_id_type=pl.DeviceIdType.MESH,
        )

    def across(d):
        return pltpu.make_async_remote_copy(
            src_ref=own_ref,
            dst_ref=held(0, 0),
            send_sem=send.at[0, d],
            recv_sem=recv.at[0, d],
            device_id=(s, flip(z, d)),
            device_id_type=pl.DeviceIdType.MESH,
        )

    even = odd == 0
    uneven = odd == 1
    both = jnp.logical_and
    sends = [
        (both(even, s + 2 < seq), lambda d: copy(own(d), 2, d, 1, 2)),
        (even, lambda d: copy(own(d), 1, d, 2, 1)),
        (both(uneven, both(pair_odd == 0, s + 2 < seq)), lambda d: copy(own(d), 2, d, 1, 2)),
        (both(uneven, s + 3 < seq), lambda d: copy(own(d), 3, d, 2, 3)),
    ]
    after_two = [
        (both(even, s >= 2), lambda d: copy(held(2, d), 3, d, 3, 1)),
        (both(uneven, s >= 2), lambda d: copy(held(2, d), 1, d, 3, -1)),
    ]
    after_three = [(both(even, both(pair_odd == 1, s >= 4)), lambda d: copy(held(3, d), 2, d, 4, -1))]
    got_two = s >= 2
    got_three_early = both(even, s >= 4)
    got_three_late = both(uneven, s >= 3)
    got_one = jnp.logical_or(uneven, s >= 2)

    def each(items, d, act):
        for holds, make in items:
            @pl.when(holds)
            def _(make=make):
                act(make(d))

    def start(items, d):
        each(items, d, lambda c: c.start())

    def arrived(holds, back, d):
        @pl.when(holds)
        def _():
            copy(own_ref, back, d, 1, 1).wait_recv()

    keep = pltpu.make_async_copy(own_ref, held(0, 0), local_sem)
    keep.start()
    for d in range(1, fsdp):
        across(d).start()
    start(sends, 0)

    def relay(d):
        arrived(got_three_early, 3, d)
        start(after_three, d)
        arrived(got_two, 2, d)
        start(after_two, d)

    for d in range(1, fsdp):
        across(d).wait_recv()
        start(sends, d)
        relay(d - 1)
    relay(fsdp - 1)
    for d in range(fsdp):
        arrived(got_three_late, 3, d)
        arrived(got_one, 1, d)
    keep.wait()
    for d in range(fsdp):
        if d:
            across(d).wait_send()
        each(sends + after_two + after_three, d, lambda c: c.wait_send())


def collect(own_kv):
    seq, fsdp = lax.axis_size("seq"), lax.axis_size("fsdp")
    rows, width = own_kv.shape
    anywhere = pl.BlockSpec(memory_space=pl.ANY)
    window = pl.pallas_call(
        functools.partial(collect_kernel, seq, fsdp),
        in_specs=[pl.BlockSpec(memory_space=pltpu.VMEM)],
        out_specs=anywhere,
        out_shape=jax.ShapeDtypeStruct((SPAN + 1, fsdp, rows, width), own_kv.dtype),
        scratch_shapes=[
            pltpu.SemaphoreType.DMA((5, fsdp)),
            pltpu.SemaphoreType.DMA((SPAN + 1, fsdp)),
            pltpu.SemaphoreType.DMA,
        ],
        compiler_params=pltpu.CompilerParams(collective_id=1, has_side_effects=True),
        name="collect",
    )(own_kv)
    return window.reshape((SPAN + 1) * fsdp * rows, width)


def local(hidden, queries, kv_weights, image_groups, doc_ids):
    rows = hidden.shape[0]
    block_rows = rows * lax.axis_size("fsdp")
    seq_place = lax.axis_index("seq")
    fsdp_place = lax.axis_index("fsdp")
    modality = image_groups[0]
    lo, hi = key_range(doc_ids, rows, block_rows, seq_place, fsdp_place, modality)
    own_kv = project(hidden, kv_weights, image_groups)
    window = collect(own_kv)
    return attend(queries, window, lo, hi)


def solution(mesh):
    in_specs = (
        P(("seq", "fsdp"), None),
        P(("seq", "fsdp"), None),
        P(None, "fsdp", None),
        P("seq"),
        P(),
    )
    out_specs = P(("seq", "fsdp"), None)
    return jax.shard_map(local, mesh=mesh, in_specs=in_specs, out_specs=out_specs, check_vma=False)
```
